32 devices in a mesh: groups: 2 (over x), ep: 16 (over z, y, core).
Axes of the slice: x: 2, y: 2, z: 4, core: 2. Of those that a mesh axis runs over, the one named last changes fastest.
Arguments:
- resid: bfloat16 [4096, 2048], P(('groups', 'ep')), parts along dimension 0, may hold values from -12 to 12
- norm_gain: float32 [2048], replicated, may hold values from 0.1 to 1.9
- expert_ids: int32 [4096, 8], P(('groups', 'ep')), parts along dimension 0, may hold values from 0 to 15, as said below
- route_weights: float32 [4096, 8], P(('groups', 'ep')), parts along dimension 0, may hold values from 0.05 to 1
- w_in: bfloat16 [16, 2048, 1536], P('ep'), may hold values from -0.125 to 0.125
- w_out: bfloat16 [16, 768, 2048], P('ep'), may hold values from -0.21875 to 0.21875
Outputs:
- layer_out: bfloat16 [4096, 2048], P(('groups', 'ep')), parts along dimension 0
The draws below stay inside these ranges and needn't reach their ends.
There are 2 independent parts, one for each index of `groups`. The reference program is written for one: setup_inputs(seed, part) draws one part's arguments, and reference() takes and returns one part's arrays. A program takes and returns all parts, laid end to end along the dimension named above; an argument that names none is the same for every part. Nothing has to cross between parts.
Inputs may be any that keep to these rules, and one draw needn't show every extreme that they name: `expert_ids`: each row names 8 different experts. Among the rows of one device no expert is named by more than 96 rows, and in every draw one expert is named by exactly 96 rows of every device.
All inputs are finite; a program needn't handle non-finite values.
Results may differ from the reference program's by a relative error of at most 0.0053.
Values may be sent and summed in bfloat16 or wider, within the bound.
A program may use at most 128 MiB of HBM per device.

```python
import math
import jax
import jax.numpy as jnp
from jax import lax

D = 2048
TOPK = 8
FF = 768
TOK_DEV = 128
EXPERTS = 16
TOKENS = 2048
CAP = 96


def draw_resid(key, part):
    first_key, second_key, third_key = jax.random.split(key, 3)
    base = jnp.clip(jax.random.normal(first_key, (TOKENS, D), jnp.float32), -4.0, 4.0)
    row_scale = jnp.exp(jax.random.uniform(second_key, (TOKENS, 1), jnp.float32, jnp.log(0.1), jnp.log(1.0)))
    column_scale = jnp.exp(jax.random.uniform(third_key, (1, D), jnp.float32, jnp.log(0.3), jnp.log(3.0)))
    return (base * row_scale * column_scale).astype(jnp.bfloat16)


def draw_expert_ids(key, part):
    blocks = TOKENS // TOK_DEV
    slot_total = EXPERTS * CAP
    chosen_count = TOK_DEV * TOPK
    favour = jax.random.randint(jax.random.fold_in(key, 11), (EXPERTS,), 0, slot_total)
    hot_expert = jax.random.randint(jax.random.fold_in(key, 12), (), 0, EXPERTS)
    expert_of = jnp.arange(slot_total, dtype=jnp.int32) // CAP
    order_key = slot_total - 1 - jnp.arange(slot_total, dtype=jnp.int32)

    def one_block(block):
        block_key = jax.random.fold_in(key, block + 100)
        noise = jax.random.randint(jax.random.fold_in(block_key, 1), (slot_total,), 0, slot_total)
        score = noise + favour[expert_of] + jnp.where(expert_of == hot_expert, 2 * slot_total, 0)
        unused, picked = lax.top_k(score * slot_total + order_key, chosen_count)
        marked = jnp.zeros((slot_total,), jnp.int32).at[picked].set(1)
        unused_too, ordered = lax.top_k(marked * slot_total + order_key, chosen_count)
        listed = (ordered // CAP).reshape(TOPK, TOK_DEV).T
        shuffle = jax.random.permutation(jax.random.fold_in(block_key, 2), TOK_DEV)
        return listed[shuffle]
    drawn = jax.vmap(one_block)(jnp.arange(blocks, dtype=jnp.int32))
    return drawn.reshape(TOKENS, TOPK).astype(jnp.int32)


def levels(stream_key, shape, cuts, smallest, top_value):
    loudness, own = 1.0, jax.random.fold_in(stream_key, 6)
    for dim, parts in cuts:
        heights = jnp.exp(jax.random.uniform(jax.random.fold_in(own, dim), (parts,), jnp.float32, smallest / len(cuts), top_value / len(cuts)))
        loudness = loudness * jnp.repeat(heights, shape[dim] // parts).reshape([-1 if axis == dim else 1 for axis in range(len(shape))])
    return loudness


def scatter_about(own_key, shape, width, limit, cuts=(), held_as=jnp.bfloat16):
    level = levels(own_key, shape, cuts, -0.22, 0.18) if cuts else 1.0
    values = jax.random.normal(own_key, shape, jnp.float32) * width * level
    return jnp.minimum(jnp.maximum(values, -limit), limit).astype(held_as)


def setup_inputs(seed: int = 0, part: int = 0) -> dict:
    key_list = jax.random.split(jax.random.key(seed), 7)
    part_keys = jax.random.split(jax.random.fold_in(key_list[6], part), 7)
    return {
        "resid": draw_resid(jax.random.fold_in(jax.random.fold_in(key_list[6], part), 71), part),
        "norm_gain": jnp.clip(1.0 + 0.18 * jax.random.normal(key_list[1], (D,), jnp.float32), 0.1, 1.9),
        "expert_ids": draw_expert_ids(jax.random.fold_in(jax.random.fold_in(key_list[6], part), 71), part),
        "route_weights": jnp.clip(jnp.exp(math.log(1.0) - 2.9957323 * jax.random.uniform(part_keys[3], (TOKENS, TOPK), jnp.float32) ** levels(part_keys[3], (TOKENS, TOPK), ((0, 16),), -0.2, 0.2)), 0.05, 1.0),
        "w_in": scatter_about(key_list[4], (EXPERTS, D, 2 * FF), D ** -0.5, 0.125, ((0, 16),)),
        "w_out": scatter_about(key_list[5], (EXPERTS, FF, D), FF ** -0.5, 0.21875, ((0, 16),)),
    }


def apply_expert(block_rows, weight_in, weight_out):
    projected = jnp.dot(block_rows, weight_in, preferred_element_type=jnp.float32)
    gate_part = projected[:, :FF]
    up_part = projected[:, FF:]
    activated = (jax.nn.silu(gate_part) * up_part).astype(jnp.bfloat16)
    return jnp.dot(activated, weight_out, preferred_element_type=jnp.float32).astype(jnp.bfloat16)

def reference(resid, norm_gain, expert_ids, route_weights, w_in, w_out):
    token_count, model_width = resid.shape
    blocks = token_count // TOK_DEV
    resid_wide = resid.astype(jnp.float32)
    scale = lax.rsqrt(lax.optimization_barrier(jnp.mean(resid_wide * resid_wide, axis=-1, keepdims=True)) + 1e-06)
    normed = (resid_wide * scale * norm_gain).astype(jnp.bfloat16)
    mix_weights = route_weights / lax.optimization_barrier(jnp.sum(route_weights, axis=-1, keepdims=True))
    flat_ids = expert_ids.reshape(blocks, TOK_DEV * TOPK).astype(jnp.int32)
    onehot = (flat_ids[:, :, None] == jnp.arange(EXPERTS, dtype=jnp.int32)[None, None, :]).astype(jnp.int32)
    position = lax.optimization_barrier(jnp.sum((jnp.cumsum(onehot, axis=1) - onehot) * onehot, axis=-1)).astype(jnp.int32)
    column = (jnp.arange(blocks, dtype=jnp.int32)[:, None] * CAP + position).astype(jnp.int32)
    token_of = jnp.repeat(jnp.arange(token_count, dtype=jnp.int32), TOPK).reshape(blocks, TOK_DEV * TOPK)
    table = jnp.zeros((EXPERTS, blocks * CAP), jnp.int32).at[flat_ids, column].set(token_of)
    weight_table = jnp.zeros((EXPERTS, blocks * CAP), jnp.float32).at[flat_ids, column].set(mix_weights.reshape(blocks, TOK_DEV * TOPK))

    def one_expert(total, inputs):
        weight_in, weight_out, token_rows, row_weights = inputs
        outputs = apply_expert(normed[token_rows], weight_in, weight_out)
        total = total.at[token_rows].add(row_weights[:, None] * outputs.astype(jnp.float32))
        return (total, None)
    total, _ = lax.scan(one_expert, jnp.zeros((token_count, model_width), jnp.float32), (w_in, w_out, table, weight_table))
    return (resid_wide + total).astype(jnp.bfloat16)
```

```python
import functools
import math

import jax
import jax.numpy as jnp
from jax import lax
from jax.experimental import pallas as pl
from jax.experimental.pallas import tpu as pltpu
from jax.sharding import PartitionSpec as P


PLANE = 4
PARTS = 2
MESH = pl.DeviceIdType.MESH
PAIRS = ("pA", "pB", "t2p")
SINGLES = ("m1", "mB", "t2", "t3", "far")

END_STEPS = (
    ("zs", 0, "01", (1, 2)), ("yc", 1), ("yc", 2), ("hand", 1), ("zs", 1, "01", (1, 3)),
    ("xa", 1), ("hand", 2), ("yc", 4), ("zz", 1, "01", (1, 3)), ("yc", 0), ("xb", 1), ("xa", 2),
    ("xb", 2), ("hand", 4), ("pair", 2, 1, "01", (1, "pA", 0)), ("xa", 4), ("yc", 6), ("hand", 0),
    ("xb", 4), ("pair", 4, 0, "01", (1, "t2p", 0)), ("yc", 7), ("yc", 5),
    ("pair", 4, 1, "01", (1, "t2p", 0)), ("hand", 6), ("xa", 6), ("xb", 6), ("hand", 7),
    ("sy", 6), ("xa", 7), ("xb", 7), ("hand", 5), ("pf", 3), ("pair", 2, 0, "01", (1, "pA", 0)),
    ("sy", 7), ("xa", 5), ("xb", 5), ("ss", 6, "01", (1, "t3", 0), None), ("c", 3), ("sy", 5),
    ("xa", 3), ("ss", 7, "01", (1, "t3", 1), None), ("xb", 3), ("sy", 3), ("sy", 1, ("pA", 1, 0)),
    ("ss", 5, "01", (1, "t2", 1), None), ("xa", 0), ("xb", 0),
    ("ss", 3, "01", (1, "m1", 1), None), ("sy", 0), ("fin", 1, ("far", 1), ("pA", 1, 1)),
    ("fin", 0, ("far", 0), ("m1", 0)),
)

INNER_STEPS = (
    ("zs", 0, "12", (1, 4)), ("zs", 0, "10", (0, 2)), ("yc", 1), ("zs", 1, "12", (1, 5)),
    ("on", 2, "12", (1, 6)), ("yc", 0), ("hand", 1), ("on", 4, "10", (0, 4)), ("yc", 2),
    ("on", 5, "10", (0, 5)), ("xa", 1), ("c", 4), ("c", 5), ("on", 3, "12", (1, 7)), ("hand", 0),
    ("xb", 1), ("yc", 6), ("on", 6, "10", (0, 6)), ("hand", 2), ("pf", 3), ("c", 3), ("xa", 2),
    ("on", 7, "10", (0, 7)), ("xb", 2), ("hand", 6), ("zz", 0, "12", (1, 4)),
    ("zz", 1, "10", (0, 3)), ("sy", 2), ("yc", 7), ("xa", 3), ("xb", 3), ("sy", 1),
    ("zs", 1, "10", (0, 3)), ("zz", 1, "12", (1, 5)), ("xa", 6), ("pf", 4), ("xb", 6), ("xa", 4),
    ("hand", 7), ("pair", 3, 0, "10", (0, "pA", 1)), ("sy", 6), ("xb", 4),
    ("ss", 2, "10", (0, "m1", 0), None), ("pair", 4, 1, "12", (1, "pB", 0), ("t2p", 0, 1)),
    ("xa", 7), ("pf", 5), ("pair", 3, 1, "10", (0, "pA", 1)), ("xb", 7), ("sy", 7),
    ("pair", 4, 0, "12", (1, "pB", 0), ("t2p", 0, 0)), ("xa", 5), ("xb", 5),
    ("ss", 6, "110", (0, "far", 0), ("t3", 0)), ("sy", 5, None), ("xa", 0), ("xb", 0),
    ("ss", 7, "110", (0, "far", 1), ("t3", 1)), ("sy", 0, ("pA", 0, 0), ("pB", 0, 0)),
    ("ss", 5, "12", (1, "mB", 1), ("t2", 1)), ("fin", 0, ("pA", 0, 1), ("pB", 0, 1)),
    ("fin", 1, ("m1", 1), ("mB", 1)),
)


def flip(index, bits):
    bit = 1
    while bit <= bits:
        if bits & bit:
            index = index + bit - 2 * bit * ((index // bit) % 2)
        bit *= 2
    return index


def moe_kernel(
    count, resid_ref, gain_ref, ids_ref, route_ref, win_hbm, wout_hbm, o_hbm,
    gathered, table_ref, weights, weight_cols, win, wout, hidden, partial, from_core, from_y,
    pair_in, single_in, out_buf,
    load_sem, out_sem, table_send, table_recv, z_send, z_recv, zz_send, zz_recv, y_send, y_recv,
    core_send, core_recv, fwd_send, fwd_recv, rc_send, rc_recv, ry_send, ry_recv,
    pair_send, pair_recv, single_send, single_recv,
):
    rows, width = resid_ref.shape
    units = wout.shape[0]
    planes = count // PLANE
    part = rows // PARTS
    tiles = rc_send.shape[1]
    me = lax.axis_index("ep")
    z, q = me // PLANE, me % PLANE
    y, c = q // 2, q % 2
    end = jnp.logical_or(z == 0, z == planes - 1)
    other_q, other_y, core_q = flip(q, 2), flip(y, 1), flip(q, 1)
    cols = (other_y, y)
    pieces = planes * PARTS
    step = 16

    def remote(src, dst, send, recv, plane, spot):
        return pltpu.make_async_remote_copy(
            src_ref=src, dst_ref=dst, send_sem=send, recv_sem=recv,
            device_id={"ep": plane * PLANE + spot}, device_id_type=MESH,
        )

    load_in = pltpu.make_async_copy(win_hbm.at[0], win, load_sem.at[0])
    load_out = pltpu.make_async_copy(wout_hbm.at[0], wout, load_sem.at[1])
    load_in.start()
    load_out.start()

    barrier = pltpu.get_barrier_semaphore()
    for k in range(1, count):
        pl.semaphore_signal(
            barrier, inc=1, device_id={"ep": lax.rem(me + k, count)}, device_id_type=MESH
        )

    for h in range(PARTS):

        @pl.loop(0, part // step)
        def _(i, h=h):
            at = pl.ds(pl.multiple_of(i * step, step), step)
            wide = resid_ref[pl.ds(pl.multiple_of(h * part + i * step, step), step), :].astype(
                jnp.float32
            )
            scale = lax.rsqrt(jnp.mean(wide * wide, axis=-1, keepdims=True) + 1e-06)
            gathered[z * PARTS + h, q, at, :] = (wide * scale * gain_ref[...]).astype(jnp.bfloat16)

    mix = route_ref[...] / jnp.sum(route_ref[...], axis=0, keepdims=True)
    for e in range(count):
        table_ref[e] = jnp.sum(jnp.where(ids_ref[...] == e, mix, 0.0), axis=0, keepdims=True)
    weights[me] = jnp.sum(jnp.where(ids_ref[...] == me, mix, 0.0), axis=0, keepdims=True)
    pl.semaphore_wait(barrier, count - 1)

    def table_copy(k):
        target = lax.rem(me + k, count)
        return pltpu.make_async_remote_copy(
            src_ref=table_ref.at[target], dst_ref=weights.at[me],
            send_sem=table_send.at[k - 1], recv_sem=table_recv.at[k - 1],
            device_id={"ep": target}, device_id_type=MESH,
        )

    for k in range(1, count):
        table_copy(k).start()

    def columns_of_weights():
        for k in range(1, count):
            table_copy(k).wait_recv()

        @pl.loop(0, count)
        def _(i):
            lane = jnp.broadcast_to(weights[i], (rows, rows))
            eye = lax.broadcasted_iota(jnp.int32, (rows, rows), 0) == lax.broadcasted_iota(
                jnp.int32, (rows, rows), 1
            )
            column = jnp.sum(jnp.where(eye, lane, 0.0), axis=1, keepdims=True)
            for h in range(PARTS):
                weight_cols[(i // PLANE) * PARTS + h, i % PLANE] = jnp.broadcast_to(
                    column[h * part : (h + 1) * part], (part, 128)
                )

    tile_in = 256 if units % 256 == 0 else units
    tile_out = width // tiles

    def play(at_end, steps):
        mate, across, beyond = flip(z, 1), flip(z, 3), flip(z, 2)
        plane_of = [z, mate, beyond, across] if at_end else [z, mate, across, beyond]
        piece_of = [plane_of[s // PARTS] * PARTS + s % PARTS for s in range(pieces)]
        to_plane = {"01": mate, "10": mate, "12": across, "012": beyond, "110": beyond}
        started, waited = [], set()

        def begin(copy):
            copy.start()
            started.append(copy)

        def own_column(s):
            return gathered.at[piece_of[s], q]

        def other_column(s):
            return gathered.at[piece_of[s], other_q]

        def tile_copy(s, j):
            at = pl.ds(pl.multiple_of(j * tile_out, 128), tile_out)
            return remote(
                partial.at[s, flip(c, 1), :, :, at], from_core.at[s, :, :, at],
                rc_send.at[s, j], rc_recv.at[s, j], z, core_q,
            )

        def arrived(name, *spot):
            if name in PAIRS:
                return pair_in.at[PAIRS.index(name), spot[0], spot[1]]
            return single_in.at[SINGLES.index(name), spot[0]]

        def wait(name, *spot):
            if (name,) + spot in waited:
                return
            waited.add((name,) + spot)
            s = spot[0]
            if name == "z":
                ref, send, recv = own_column(s), z_send.at[0], z_recv.at[piece_of[s]]
            elif name == "zz":
                ref, send, recv = other_column(s), zz_send.at[0], zz_recv.at[s]
            elif name == "y":
                ref, send, recv = own_column(s), y_send.at[s], y_recv.at[s]
            elif name == "c":
                ref, send, recv = own_column(s), core_send.at[s], core_recv.at[s]
            elif name == "f":
                ref, send, recv = other_column(s), fwd_send.at[s], fwd_recv.at[s]
            elif name == "ry":
                ref, send, recv = from_y.at[s], ry_send.at[s], ry_recv.at[s]
            elif name in PAIRS:
                kind = PAIRS.index(name)
                ref = arrived(name, *spot)
                send, recv = pair_send.at[0], pair_recv.at[kind, spot[0], spot[1]]
            elif name in SINGLES:
                kind = SINGLES.index(name)
                ref = arrived(name, *spot)
                send, recv = single_send.at[0], single_recv.at[kind, spot[0]]
            else:
                for j in range(tiles):
                    tile_copy(s, j).wait_recv()
                return
            remote(ref, ref, send, recv, z, core_q).wait_recv()

        def core(s):
            begin(
                remote(
                    own_column(s), own_column(s), core_send.at[s], core_recv.at[s], z, core_q
                )
            )

        def hand(s):
            begin(
                remote(
                    other_column(s), other_column(s), fwd_send.at[s], fwd_recv.at[s], z, core_q
                )
            )

        def add_rows(store, loads):
            @pl.loop(0, part // step)
            def _(i):
                at = pl.ds(pl.multiple_of(i * step, step), step)
                total = loads[0][at, :].astype(jnp.float32)
                for ref in loads[1:]:
                    total = total + ref[at, :].astype(jnp.float32)
                store[at, :] = total.astype(jnp.bfloat16)

        def sums(s, side, extras):
            wait("rc", s)
            spot = partial.at[s, c, cols[side]]
            loads = [spot, from_core.at[s, cols[side]]]
            for extra in extras:
                wait(*extra)
                loads.append(from_y.at[s] if extra[0] == "ry" else arrived(*extra))
            add_rows(spot, loads)
            return spot

        def first_matmul(s):
            @pl.loop(0, units // tile_in)
            def _(j):
                gate_at = pl.multiple_of(j * tile_in, 128)
                up_at = pl.multiple_of(units + j * tile_in, 128)
                block = gathered[piece_of[s]].reshape(PLANE * part, width)
                gate = jnp.dot(
                    block, win[:, pl.ds(gate_at, tile_in)], preferred_element_type=jnp.float32
                )
                up = jnp.dot(
                    block, win[:, pl.ds(up_at, tile_in)], preferred_element_type=jnp.float32
                )
                act = gate / (1.0 + jnp.exp(-gate)) * up
                hidden[:, pl.ds(gate_at, tile_in)] = act.astype(jnp.bfloat16)

        def second_matmul(s):
            @pl.loop(0, tiles)
            def _(j):
                at = pl.multiple_of(j * tile_out, 128)
                made = jnp.dot(
                    hidden[...], wout[:, pl.ds(at, tile_out)], preferred_element_type=jnp.float32
                )
                made = made.astype(jnp.bfloat16).astype(jnp.float32)
                for k in range(PLANE):
                    scale = weight_cols[piece_of[s], k]
                    scaled = [
                        made[k * part : (k + 1) * part, i * 128 : (i + 1) * 128] * scale
                        for i in range(tile_out // 128)
                    ]
                    partial[s, k % 2, k // 2, :, pl.ds(at, tile_out)] = jnp.concatenate(
                        scaled, axis=1
                    ).astype(jnp.bfloat16)
                tile_copy(s, j).start()

        def finish(h, extras):
            wait("rc", h)
            wait("ry", h)
            refs = [from_core.at[h, y], from_y.at[h]]
            for extra in extras:
                wait(*extra)
                refs.append(arrived(*extra))

            @pl.loop(0, part // step)
            def _(i):
                at = pl.ds(pl.multiple_of(i * step, step), step)
                out_at = pl.ds(pl.multiple_of(h * part + i * step, step), step)
                total = partial[h, c, y, at, :].astype(jnp.float32)
                for ref in refs:
                    total = total + ref[at, :].astype(jnp.float32)
                out_buf[out_at, :] = (resid_ref[out_at, :].astype(jnp.float32) + total).astype(
                    jnp.bfloat16
                )

            out_at = pl.ds(h * part, part)
            pltpu.make_async_copy(
                out_buf.at[out_at, :], o_hbm.at[out_at, :], out_sem.at[h]
            ).start()

        z_count = zz_count = pair_count = single_count = 0
        loaded = False
        for item in steps:
            kind, s = item[0], item[1]
            if kind in ("zs", "on"):
                if kind == "on":
                    wait("z", s)
                begin(
                    remote(
                        own_column(s), own_column(s), z_send.at[z_count],
                        z_recv.at[piece_of[s]], to_plane[item[2]], q,
                    )
                )
                z_count += 1
            elif kind in ("yc", "c"):
                if s >= PARTS:
                    wait("z", s)
                if kind == "yc":
                    begin(
                        remote(
                            own_column(s), own_column(s), y_send.at[s], y_recv.at[s], z, other_q
                        )
                    )
                core(s)
            elif kind == "hand":
                wait("y", s)
                hand(s)
            elif kind == "pf":
                wait("zz", s)
                hand(s)
            elif kind == "zz":
                wait("y", s)
                begin(
                    remote(
                        other_column(s), other_column(s), zz_send.at[zz_count],
                        zz_recv.at[item[3][1]], to_plane[item[2]], q,
                    )
                )
                zz_count += 1
            elif kind == "xa":
                wait("c", s)
                wait("f", s)
                if not loaded:
                    columns_of_weights()
                    load_in.wait()
                    load_out.wait()
                    loaded = True
                first_matmul(s)
            elif kind == "xb":
                second_matmul(s)
            elif kind == "sy":
                spot = sums(s, 0, [extra for extra in item[2:] if extra])
                begin(remote(spot, from_y.at[s], ry_send.at[s], ry_recv.at[s], z, other_q))
            elif kind == "ss":
                spot = sums(s, 1, [("ry", s)] + [extra for extra in item[4:] if extra])
                where = (SINGLES.index(item[3][1]), item[3][2])
                begin(
                    remote(
                        spot, single_in.at[where[0], where[1]], single_send.at[single_count],
                        single_recv.at[where[0], where[1]], to_plane[item[2]], q,
                    )
                )
                single_count += 1
            elif kind == "pair":
                side = item[2]
                spot = sums(s, side, [extra for extra in item[5:] if extra])
                where = (PAIRS.index(item[4][1]), item[4][2], side)
                begin(
                    remote(
                        spot, pair_in.at[where], pair_send.at[pair_count],
                        pair_recv.at[where], to_plane[item[3]], q,
                    )
                )
                pair_count += 1
            else:
                finish(s, item[2:])
        for copy in started:
            copy.wait_send()
        for s in range(pieces):
            for j in range(tiles):
                tile_copy(s, j).wait_send()

    @pl.when(end)
    def _():
        play(True, END_STEPS)

    @pl.when(jnp.logical_not(end))
    def _():
        play(False, INNER_STEPS)

    for k in range(1, count):
        table_copy(k).wait_send()
    for h in range(PARTS):
        at = pl.ds(h * part, part)
        pltpu.make_async_copy(out_buf.at[at, :], o_hbm.at[at, :], out_sem.at[h]).wait()


def local(resid, norm_gain, expert_ids, route_weights, w_in, w_out):
    rows, width = resid.shape
    units = w_out.shape[1]
    count = lax.axis_size("ep")
    planes = count // PLANE
    part, pieces, tiles = rows // PARTS, planes * PARTS, 4
    bf16 = jnp.bfloat16
    blocks = [
        (pieces, PLANE, part, width), (pieces, 2, 2, part, width), (pieces, 2, part, width),
        (pieces, part, width), (len(PAIRS), PARTS, 2, part, width),
        (len(SINGLES), PARTS, part, width), (rows, width), (width, 2 * units), (units, width),
        (PLANE * part, units),
    ]
    vmem_bytes = sum(2 * math.prod(shape) for shape in blocks) + 4 * 128 * PLANE * part * pieces
    if planes != 4 or count != 16 or rows != 128 or width % 512 or vmem_bytes > 50 * 2**20:
        return local_wide(resid, norm_gain, expert_ids, route_weights, w_in, w_out)
    vmem = pl.BlockSpec(memory_space=pltpu.VMEM)
    hbm = pl.BlockSpec(memory_space=pl.ANY)
    dma = pltpu.SemaphoreType.DMA
    (gathered, partial, from_core, from_y, pair_in, single_in, out_buf, win, wout, hidden) = [
        pltpu.VMEM(shape, bf16) for shape in blocks
    ]
    table = pltpu.VMEM((count, 1, rows), jnp.float32)
    columns = pltpu.VMEM((pieces, PLANE, part, 128), jnp.float32)
    return pl.pallas_call(
        functools.partial(moe_kernel, count),
        out_shape=jax.ShapeDtypeStruct((rows, width), bf16),
        in_specs=[vmem, vmem, vmem, vmem, hbm, hbm],
        out_specs=hbm,
        scratch_shapes=[
            gathered, table, table, columns, win, wout, hidden, partial, from_core, from_y,
            pair_in, single_in, out_buf,
            dma((2,)), dma((PARTS,)), dma((count - 1,)), dma((count - 1,)),
            dma((2 * pieces,)), dma((pieces,)), dma((pieces,)), dma((pieces,)),
        ]
        + [dma((pieces,))] * 6
        + [dma((pieces, tiles))] * 2
        + [dma((pieces,))] * 2
        + [dma((4 * pieces,)), dma((len(PAIRS), PARTS, 2))]
        + [dma((2 * pieces,)), dma((len(SINGLES), PARTS))],
        compiler_params=pltpu.CompilerParams(
            collective_id=0, has_side_effects=True, vmem_limit_bytes=60 * 2**20
        ),
    )(resid, norm_gain[None], expert_ids.T, route_weights.T, w_in, w_out)


def local_wide(resid, norm_gain, expert_ids, route_weights, w_in, w_out):
    token_rows, model_width = resid.shape
    top_count = expert_ids.shape[1]
    ep_devices = lax.axis_size("ep")
    capacity = 3 * token_rows * top_count // (2 * ep_devices)
    weight_in = w_in[0]
    weight_out = w_out[0]
    hidden_units = weight_out.shape[0]
    resid_wide = resid.astype(jnp.float32)
    scale = lax.rsqrt(jnp.mean(resid_wide * resid_wide, axis=-1, keepdims=True) + 1e-06)
    normed = (resid_wide * scale * norm_gain).astype(jnp.bfloat16)
    mix_weights = route_weights / jnp.sum(route_weights, axis=-1, keepdims=True)
    flat_ids = expert_ids.reshape(-1)
    onehot = (flat_ids[:, None] == jnp.arange(ep_devices, dtype=jnp.int32)[None, :]).astype(
        jnp.int32
    )
    position = jnp.sum((jnp.cumsum(onehot, axis=0) - onehot) * onehot, axis=1)
    slot_index = flat_ids * capacity + position
    all_normed, all_ids = (
        lax.all_gather(normed, "ep", axis=0, tiled=True),
        lax.all_gather(expert_ids, "ep", axis=0, tiled=True),
    )
    own_expert = lax.axis_index("ep")
    row_hits = (
        jnp.any(all_ids == own_expert, axis=1).astype(jnp.int32).reshape(ep_devices, token_rows)
    )
    placing = jnp.cumsum(row_hits, axis=1) - row_hits
    target = jnp.where(
        row_hits == 1,
        jnp.arange(ep_devices, dtype=jnp.int32)[:, None] * capacity + placing,
        ep_devices * capacity,
    ).reshape(-1)
    received = (
        jnp.zeros((ep_devices * capacity, model_width), jnp.bfloat16)
        .at[target]
        .set(all_normed, mode="drop")
    )
    block_rows = received.reshape(ep_devices, capacity, model_width)
    rows_flat = block_rows.reshape(-1, model_width)
    projected = jnp.dot(rows_flat, weight_in, preferred_element_type=jnp.float32)
    activated = (jax.nn.silu(projected[:, :hidden_units]) * projected[:, hidden_units:]).astype(
        jnp.bfloat16
    )
    produced = jnp.dot(activated, weight_out, preferred_element_type=jnp.float32).astype(
        jnp.bfloat16
    )
    outputs = produced.reshape(block_rows.shape)
    returned = lax.all_to_all(outputs, "ep", split_axis=0, concat_axis=0, tiled=True).reshape(
        -1, model_width
    )
    picked = returned[slot_index].reshape(token_rows, top_count, model_width).astype(jnp.float32)
    mixed = jnp.sum(mix_weights[:, :, None] * picked, axis=1)
    return (resid_wide + mixed).astype(jnp.bfloat16)


def solution(mesh):
    in_specs = (
        P(("groups", "ep"), None),
        P(),
        P(("groups", "ep"), None),
        P(("groups", "ep"), None),
        P("ep", None, None),
        P("ep", None, None),
    )
    out_specs = P(("groups", "ep"), None)
    return jax.shard_map(local, mesh=mesh, in_specs=in_specs, out_specs=out_specs, check_vma=False)
```

```python
import functools
import math

import jax
import jax.numpy as jnp
from jax import lax
from jax.experimental import pallas as pl
from jax.experimental.pallas import tpu as pltpu
from jax.sharding import PartitionSpec as P


PLANE = 4
PARTS = 2
MESH = pl.DeviceIdType.MESH
PAIRS = ("pA", "pB", "t2p")
SINGLES = ("m1", "mB", "t2", "t3", "far")

END_STEPS = (
    ("yc", 0), ("zs", 0, "01", (1, 2)), ("zs", 1, "01", (1, 3)), ("yc", 1), ("yc", 2),
    ("hand", 0), ("hand", 1), ("zz", 1, "01", (1, 3)), ("xa", 0), ("yc", 4), ("xb", 0),
    ("hand", 2), ("xa", 2), ("yc", 6), ("xb", 2), ("hand", 4), ("pair", 2, 0, "01", (1, "pA", 0)),
    ("pair", 2, 1, "01", (1, "pA", 0)), ("yc", 7), ("xa", 4), ("hand", 6), ("xb", 4), ("xa", 6),
    ("yc", 5), ("xb", 6), ("hand", 7), ("pair", 4, 1, "01", (1, "t2p", 0)),
    ("pair", 4, 0, "01", (1, "t2p", 0)), ("sy", 6), ("xa", 7), ("xb", 7), ("hand", 5), ("sy", 7),
    ("xa", 5), ("c", 3), ("pf", 3), ("xb", 5), ("ss", 6, "01", (1, "t3", 0), None), ("sy", 5),
    ("xa", 3), ("ss", 7, "01", (1, "t3", 1), None), ("xb", 3), ("sy", 3),
    ("ss", 5, "01", (1, "t2", 1), None), ("xa", 1), ("sy", 0), ("xb", 1), ("sy", 1),
    ("ss", 3, "01", (1, "m1", 1), None), ("fin", 0, ("far", 0), ("m1", 0)),
    ("fin", 1, ("far", 1), ("m1", 1)),
)

INNER_STEPS = (
    ("yc", 1), ("zs", 0, "12", (1, 4)), ("zs", 0, "10", (0, 2)), ("on", 4, "10", (0, 4)),
    ("on", 2, "12", (1, 6)), ("hand", 1), ("yc", 2), ("xa", 1), ("on", 3, "12", (1, 7)),
    ("yc", 0), ("on", 6, "10", (0, 6)), ("hand", 2), ("xb", 1), ("xa", 2), ("yc", 6), ("c", 4),
    ("c", 3), ("zs", 1, "12", (1, 5)), ("pf", 3), ("on", 7, "10", (0, 7)), ("yc", 7), ("xb", 2),
    ("xa", 3), ("zz", 1, "12", (1, 5)), ("on", 5, "10", (0, 5)), ("xb", 3),
    ("zs", 1, "10", (0, 3)), ("hand", 0), ("sy", 3), ("hand", 6), ("c", 5),
    ("zz", 1, "10", (0, 3)), ("sy", 2), ("zz", 0, "12", (1, 4)), ("xa", 6), ("xb", 6), ("sy", 6),
    ("pf", 4), ("hand", 7), ("sy", 1), ("xa", 4), ("pf", 5), ("xb", 4),
    ("ss", 3, "10", (0, "m1", 1), None), ("pair", 4, 1, "12", (1, "pB", 0), ("t2p", 0, 1)),
    ("ss", 2, "10", (0, "m1", 0), None), ("xa", 7), ("xb", 7),
    ("pair", 4, 0, "12", (1, "pB", 0), ("t2p", 0, 0)), ("xa", 5), ("sy", 7), ("xb", 5),
    ("ss", 6, "110", (0, "far", 0), ("t3", 0)), ("sy", 5, None), ("xa", 0), ("xb", 0),
    ("ss", 7, "110", (0, "far", 1), ("t3", 1)), ("sy", 0, ("pA", 0, 0), ("pB", 0, 0)),
    ("ss", 5, "12", (1, "mB", 1), ("t2", 1)), ("fin", 0, ("pA", 0, 1), ("pB", 0, 1)),
    ("fin", 1, ("m1", 1), ("mB", 1)),
)


def flip(index, bits):
    bit = 1
    while bit <= bits:
        if bits & bit:
            index = index + bit - 2 * bit * ((index // bit) % 2)
        bit *= 2
    return index


def moe_kernel(
    count, resid_ref, gain_ref, ids_ref, route_ref, win_hbm, wout_hbm, o_hbm,
    gathered, table_ref, weights, weight_cols, win, wout, hidden, partial, from_core, from_y,
    pair_in, single_in, out_buf,
    load_sem, out_sem, table_send, table_recv, z_send, z_recv, zz_send, zz_recv, y_send, y_recv,
    core_send, core_recv, fwd_send, fwd_recv, rc_send, rc_recv, ry_send, ry_recv,
    pair_send, pair_recv, single_send, single_recv,
):
    rows, width = resid_ref.shape
    units = wout.shape[0]
    planes = count // PLANE
    part = rows // PARTS
    tiles = rc_send.shape[1]
    me = lax.axis_index("ep")
    z, q = me // PLANE, me % PLANE
    y, c = q // 2, q % 2
    end = jnp.logical_or(z == 0, z == planes - 1)
    other_q, other_y, core_q = flip(q, 2), flip(y, 1), flip(q, 1)
    cols = (other_y, y)
    pieces = planes * PARTS
    step = 16

    def remote(src, dst, send, recv, plane, spot):
        return pltpu.make_async_remote_copy(
            src_ref=src, dst_ref=dst, send_sem=send, recv_sem=recv,
            device_id={"ep": plane * PLANE + spot}, device_id_type=MESH,
        )

    load_in = pltpu.make_async_copy(win_hbm.at[0], win, load_sem.at[0])
    load_out = pltpu.make_async_copy(wout_hbm.at[0], wout, load_sem.at[1])
    load_in.start()
    load_out.start()

    barrier = pltpu.get_barrier_semaphore()
    for k in range(1, count):
        pl.semaphore_signal(
            barrier, inc=1, device_id={"ep": lax.rem(me + k, count)}, device_id_type=MESH
        )

    for h in range(PARTS):

        @pl.loop(0, part // step)
        def _(i, h=h):
            at = pl.ds(pl.multiple_of(i * step, step), step)
            wide = resid_ref[pl.ds(pl.multiple_of(h * part + i * step, step), step), :].astype(
                jnp.float32
            )
            scale = lax.rsqrt(jnp.mean(wide * wide, axis=-1, keepdims=True) + 1e-06)
            gathered[z * PARTS + h, q, at, :] = (wide * scale * gain_ref[...]).astype(jnp.bfloat16)

    mix = route_ref[...] / jnp.sum(route_ref[...], axis=0, keepdims=True)
    for e in range(count):
        table_ref[e] = jnp.sum(jnp.where(ids_ref[...] == e, mix, 0.0), axis=0, keepdims=True)
    weights[me] = jnp.sum(jnp.where(ids_ref[...] == me, mix, 0.0), axis=0, keepdims=True)
    pl.semaphore_wait(barrier, count - 1)

    def table_copy(k):
        target = lax.rem(me + k, count)
        return pltpu.make_async_remote_copy(
            src_ref=table_ref.at[target], dst_ref=weights.at[me],
            send_sem=table_send.at[k - 1], recv_sem=table_recv.at[k - 1],
            device_id={"ep": target}, device_id_type=MESH,
        )

    for k in range(1, count):
        table_copy(k).start()

    def columns_of_weights():
        for k in range(1, count):
            table_copy(k).wait_recv()

        @pl.loop(0, count)
        def _(i):
            lane = jnp.broadcast_to(weights[i], (rows, rows))
            eye = lax.broadcasted_iota(jnp.int32, (rows, rows), 0) == lax.broadcasted_iota(
                jnp.int32, (rows, rows), 1
            )
            column = jnp.sum(jnp.where(eye, lane, 0.0), axis=1, keepdims=True)
            for h in range(PARTS):
                weight_cols[(i // PLANE) * PARTS + h, i % PLANE] = jnp.broadcast_to(
                    column[h * part : (h + 1) * part], (part, 128)
                )

    tile_in = 256 if units % 256 == 0 else units
    tile_out = width // tiles

    def play(at_end, steps):
        mate, across, beyond = flip(z, 1), flip(z, 3), flip(z, 2)
        plane_of = [z, mate, beyond, across] if at_end else [z, mate, across, beyond]
        piece_of = [plane_of[s // PARTS] * PARTS + s % PARTS for s in range(pieces)]
        to_plane = {"01": mate, "10": mate, "12": across, "012": beyond, "110": beyond}
        started, waited = [], set()

        def begin(copy):
            copy.start()
            started.append(copy)

        def own_column(s):
            return gathered.at[piece_of[s], q]

        def other_column(s):
            return gathered.at[piece_of[s], other_q]

        def tile_copy(s, j):
            at = pl.ds(pl.multiple_of(j * tile_out, 128), tile_out)
            return remote(
                partial.at[s, flip(c, 1), :, :, at], from_core.at[s, :, :, at],
                rc_send.at[s, j], rc_recv.at[s, j], z, core_q,
            )

        def arrived(name, *spot):
            if name in PAIRS:
                return pair_in.at[PAIRS.index(name), spot[0], spot[1]]
            return single_in.at[SINGLES.index(name), spot[0]]

        def wait(name, *spot):
            if (name,) + spot in waited:
                return
            waited.add((name,) + spot)
            s = spot[0]
            if name == "z":
                ref, send, recv = own_column(s), z_send.at[0], z_recv.at[piece_of[s]]
            elif name == "zz":
                ref, send, recv = other_column(s), zz_send.at[0], zz_recv.at[s]
            elif name == "y":
                ref, send, recv = own_column(s), y_send.at[s], y_recv.at[s]
            elif name == "c":
                ref, send, recv = own_column(s), core_send.at[s], core_recv.at[s]
            elif name == "f":
                ref, send, recv = other_column(s), fwd_send.at[s], fwd_recv.at[s]
            elif name == "ry":
                ref, send, recv = from_y.at[s], ry_send.at[s], ry_recv.at[s]
            elif name in PAIRS:
                kind = PAIRS.index(name)
                ref = arrived(name, *spot)
                send, recv = pair_send.at[0], pair_recv.at[kind, spot[0], spot[1]]
            elif name in SINGLES:
                kind = SINGLES.index(name)
                ref = arrived(name, *spot)
                send, recv = single_send.at[0], single_recv.at[kind, spot[0]]
            else:
                for j in range(tiles):
                    tile_copy(s, j).wait_recv()
                return
            remote(ref, ref, send, recv, z, core_q).wait_recv()

        def core(s):
            begin(
                remote(
                    own_column(s), own_column(s), core_send.at[s], core_recv.at[s], z, core_q
                )
            )

        def hand(s):
            begin(
                remote(
                    other_column(s), other_column(s), fwd_send.at[s], fwd_recv.at[s], z, core_q
                )
            )

        def add_rows(store, loads):
            @pl.loop(0, part // step)
            def _(i):
                at = pl.ds(pl.multiple_of(i * step, step), step)
                total = loads[0][at, :].astype(jnp.float32)
                for ref in loads[1:]:
                    total = total + ref[at, :].astype(jnp.float32)
                store[at, :] = total.astype(jnp.bfloat16)

        def sums(s, side, extras):
            wait("rc", s)
            spot = partial.at[s, c, cols[side]]
            loads = [spot, from_core.at[s, cols[side]]]
            for extra in extras:
                wait(*extra)
                loads.append(from_y.at[s] if extra[0] == "ry" else arrived(*extra))
            add_rows(spot, loads)
            return spot

        def first_matmul(s):
            @pl.loop(0, units // tile_in)
            def _(j):
                gate_at = pl.multiple_of(j * tile_in, 128)
                up_at = pl.multiple_of(units + j * tile_in, 128)
                block = gathered[piece_of[s]].reshape(PLANE * part, width)
                gate = jnp.dot(
                    block, win[:, pl.ds(gate_at, tile_in)], preferred_element_type=jnp.float32
                )
                up = jnp.dot(
                    block, win[:, pl.ds(up_at, tile_in)], preferred_element_type=jnp.float32
                )
                act = gate / (1.0 + jnp.exp(-gate)) * up
                hidden[:, pl.ds(gate_at, tile_in)] = act.astype(jnp.bfloat16)

        def second_matmul(s):
            @pl.loop(0, tiles)
            def _(j):
                at = pl.multiple_of(j * tile_out, 128)
                made = jnp.dot(
                    hidden[...], wout[:, pl.ds(at, tile_out)], preferred_element_type=jnp.float32
                )
                made = made.astype(jnp.bfloat16).astype(jnp.float32)
                for k in range(PLANE):
                    scale = weight_cols[piece_of[s], k]
                    scaled = [
                        made[k * part : (k + 1) * part, i * 128 : (i + 1) * 128] * scale
                        for i in range(tile_out // 128)
                    ]
                    partial[s, k % 2, k // 2, :, pl.ds(at, tile_out)] = jnp.concatenate(
                        scaled, axis=1
                    ).astype(jnp.bfloat16)
                tile_copy(s, j).start()

        def finish(h, extras):
            wait("rc", h)
            wait("ry", h)
            refs = [from_core.at[h, y], from_y.at[h]]
            for extra in extras:
                wait(*extra)
                refs.append(arrived(*extra))

            @pl.loop(0, part // step)
            def _(i):
                at = pl.ds(pl.multiple_of(i * step, step), step)
                out_at = pl.ds(pl.multiple_of(h * part + i * step, step), step)
                total = partial[h, c, y, at, :].astype(jnp.float32)
                for ref in refs:
                    total = total + ref[at, :].astype(jnp.float32)
                out_buf[out_at, :] = (resid_ref[out_at, :].astype(jnp.float32) + total).astype(
                    jnp.bfloat16
                )

            out_at = pl.ds(h * part, part)
            pltpu.make_async_copy(
                out_buf.at[out_at, :], o_hbm.at[out_at, :], out_sem.at[h]
            ).start()

        z_count = zz_count = pair_count = single_count = 0
        loaded = False
        for item in steps:
            kind, s = item[0], item[1]
            if kind in ("zs", "on"):
                if kind == "on":
                    wait("z", s)
                begin(
                    remote(
                        own_column(s), own_column(s), z_send.at[z_count],
                        z_recv.at[piece_of[s]], to_plane[item[2]], q,
                    )
                )
                z_count += 1
            elif kind in ("yc", "c"):
                if s >= PARTS:
                    wait("z", s)
                if kind == "yc":
                    begin(
                        remote(
                            own_column(s), own_column(s), y_send.at[s], y_recv.at[s], z, other_q
                        )
                    )
                core(s)
            elif kind == "hand":
                wait("y", s)
                hand(s)
            elif kind == "pf":
                wait("zz", s)
                hand(s)
            elif kind == "zz":
                wait("y", s)
                begin(
                    remote(
                        other_column(s), other_column(s), zz_send.at[zz_count],
                        zz_recv.at[item[3][1]], to_plane[item[2]], q,
                    )
                )
                zz_count += 1
            elif kind == "xa":
                wait("c", s)
                wait("f", s)
                if not loaded:
                    columns_of_weights()
                    load_in.wait()
                    load_out.wait()
                    loaded = True
                first_matmul(s)
            elif kind == "xb":
                second_matmul(s)
            elif kind == "sy":
                spot = sums(s, 0, [extra for extra in item[2:] if extra])
                begin(remote(spot, from_y.at[s], ry_send.at[s], ry_recv.at[s], z, other_q))
            elif kind == "ss":
                spot = sums(s, 1, [("ry", s)] + [extra for extra in item[4:] if extra])
                where = (SINGLES.index(item[3][1]), item[3][2])
                begin(
                    remote(
                        spot, single_in.at[where[0], where[1]], single_send.at[single_count],
                        single_recv.at[where[0], where[1]], to_plane[item[2]], q,
                    )
                )
                single_count += 1
            elif kind == "pair":
                side = item[2]
                spot = sums(s, side, [extra for extra in item[5:] if extra])
                where = (PAIRS.index(item[4][1]), item[4][2], side)
                begin(
                    remote(
                        spot, pair_in.at[where], pair_send.at[pair_count],
                        pair_recv.at[where], to_plane[item[3]], q,
                    )
                )
                pair_count += 1
            else:
                finish(s, item[2:])
        for copy in started:
            copy.wait_send()
        for s in range(pieces):
            for j in range(tiles):
                tile_copy(s, j).wait_send()

    @pl.when(end)
    def _():
        play(True, END_STEPS)

    @pl.when(jnp.logical_not(end))
    def _():
        play(False, INNER_STEPS)

    for k in range(1, count):
        table_copy(k).wait_send()
    for h in range(PARTS):
        at = pl.ds(h * part, part)
        pltpu.make_async_copy(out_buf.at[at, :], o_hbm.at[at, :], out_sem.at[h]).wait()


def local(resid, norm_gain, expert_ids, route_weights, w_in, w_out):
    rows, width = resid.shape
    units = w_out.shape[1]
    count = lax.axis_size("ep")
    planes = count // PLANE
    part, pieces, tiles = rows // PARTS, planes * PARTS, 4
    bf16 = jnp.bfloat16
    blocks = [
        (pieces, PLANE, part, width), (pieces, 2, 2, part, width), (pieces, 2, part, width),
        (pieces, part, width), (len(PAIRS), PARTS, 2, part, width),
        (len(SINGLES), PARTS, part, width), (rows, width), (width, 2 * units), (units, width),
        (PLANE * part, units),
    ]
    vmem_bytes = sum(2 * math.prod(shape) for shape in blocks) + 4 * 128 * PLANE * part * pieces
    if planes != 4 or count != 16 or rows != 128 or width % 512 or vmem_bytes > 50 * 2**20:
        return local_wide(resid, norm_gain, expert_ids, route_weights, w_in, w_out)
    vmem = pl.BlockSpec(memory_space=pltpu.VMEM)
    hbm = pl.BlockSpec(memory_space=pl.ANY)
    dma = pltpu.SemaphoreType.DMA
    (gathered, partial, from_core, from_y, pair_in, single_in, out_buf, win, wout, hidden) = [
        pltpu.VMEM(shape, bf16) for shape in blocks
    ]
    table = pltpu.VMEM((count, 1, rows), jnp.float32)
    columns = pltpu.VMEM((pieces, PLANE, part, 128), jnp.float32)
    return pl.pallas_call(
        functools.partial(moe_kernel, count),
        out_shape=jax.ShapeDtypeStruct((rows, width), bf16),
        in_specs=[vmem, vmem, vmem, vmem, hbm, hbm],
        out_specs=hbm,
        scratch_shapes=[
            gathered, table, table, columns, win, wout, hidden, partial, from_core, from_y,
            pair_in, single_in, out_buf,
            dma((2,)), dma((PARTS,)), dma((count - 1,)), dma((count - 1,)),
            dma((2 * pieces,)), dma((pieces,)), dma((pieces,)), dma((pieces,)),
        ]
        + [dma((pieces,))] * 6
        + [dma((pieces, tiles))] * 2
        + [dma((pieces,))] * 2
        + [dma((4 * pieces,)), dma((len(PAIRS), PARTS, 2))]
        + [dma((2 * pieces,)), dma((len(SINGLES), PARTS))],
        compiler_params=pltpu.CompilerParams(
            collective_id=0, has_side_effects=True, vmem_limit_bytes=60 * 2**20
        ),
    )(resid, norm_gain[None], expert_ids.T, route_weights.T, w_in, w_out)


def local_wide(resid, norm_gain, expert_ids, route_weights, w_in, w_out):
    token_rows, model_width = resid.shape
    top_count = expert_ids.shape[1]
    ep_devices = lax.axis_size("ep")
    capacity = 3 * token_rows * top_count // (2 * ep_devices)
    weight_in = w_in[0]
    weight_out = w_out[0]
    hidden_units = weight_out.shape[0]
    resid_wide = resid.astype(jnp.float32)
    scale = lax.rsqrt(jnp.mean(resid_wide * resid_wide, axis=-1, keepdims=True) + 1e-06)
    normed = (resid_wide * scale * norm_gain).astype(jnp.bfloat16)
    mix_weights = route_weights / jnp.sum(route_weights, axis=-1, keepdims=True)
    flat_ids = expert_ids.reshape(-1)
    onehot = (flat_ids[:, None] == jnp.arange(ep_devices, dtype=jnp.int32)[None, :]).astype(
        jnp.int32
    )
    position = jnp.sum((jnp.cumsum(onehot, axis=0) - onehot) * onehot, axis=1)
    slot_index = flat_ids * capacity + position
    all_normed, all_ids = (
        lax.all_gather(normed, "ep", axis=0, tiled=True),
        lax.all_gather(expert_ids, "ep", axis=0, tiled=True),
    )
    own_expert = lax.axis_index("ep")
    row_hits = (
        jnp.any(all_ids == own_expert, axis=1).astype(jnp.int32).reshape(ep_devices, token_rows)
    )
    placing = jnp.cumsum(row_hits, axis=1) - row_hits
    target = jnp.where(
        row_hits == 1,
        jnp.arange(ep_devices, dtype=jnp.int32)[:, None] * capacity + placing,
        ep_devices * capacity,
    ).reshape(-1)
    received = (
        jnp.zeros((ep_devices * capacity, model_width), jnp.bfloat16)
        .at[target]
        .set(all_normed, mode="drop")
    )
    block_rows = received.reshape(ep_devices, capacity, model_width)
    rows_flat = block_rows.reshape(-1, model_width)
    projected = jnp.dot(rows_flat, weight_in, preferred_element_type=jnp.float32)
    activated = (jax.nn.silu(projected[:, :hidden_units]) * projected[:, hidden_units:]).astype(
        jnp.bfloat16
    )
    produced = jnp.dot(activated, weight_out, preferred_element_type=jnp.float32).astype(
        jnp.bfloat16
    )
    outputs = produced.reshape(block_rows.shape)
    returned = lax.all_to_all(outputs, "ep", split_axis=0, concat_axis=0, tiled=True).reshape(
        -1, model_width
    )
    picked = returned[slot_index].reshape(token_rows, top_count, model_width).astype(jnp.float32)
    mixed = jnp.sum(mix_weights[:, :, None] * picked, axis=1)
    return (resid_wide + mixed).astype(jnp.bfloat16)


def solution(mesh):
    in_specs = (
        P(("groups", "ep"), None),
        P(),
        P(("groups", "ep"), None),
        P(("groups", "ep"), None),
        P("ep", None, None),
        P("ep", None, None),
    )
    out_specs = P(("groups", "ep"), None)
    return jax.shard_map(local, mesh=mesh, in_specs=in_specs, out_specs=out_specs, check_vma=False)
```
